32 devices in a mesh: fsdp: 4 (over x, core), context: 8 (over z, y).
Axes of the slice: x: 2, y: 2, z: 4, core: 2. Of those that a mesh axis runs over, the one named last changes fastest.
Arguments:
- block_table: int32 [8, 2], replicated, may hold values from 0 to 15, as said below
- block_input: bfloat16 [4, 1024, 2304], P('fsdp', 'context'), may hold values from -6 to 6
- output_grad: bfloat16 [4, 1024, 2304], P('fsdp', 'context'), may hold values from -6 to 6
- query_weight: bfloat16 [2304, 2048], P('fsdp'), may hold values from -0.125 to 0.125
- key_weight: bfloat16 [2304, 1024], P('fsdp'), may hold values from -0.125 to 0.125
- value_weight: bfloat16 [2304, 1024], P('fsdp'), may hold values from -0.125 to 0.125
- output_weight: bfloat16 [2048, 2304], P('fsdp'), may hold values from -0.125 to 0.125
- gate_weight: bfloat16 [2304, 9216], P('fsdp'), may hold values from -0.125 to 0.125
- up_weight: bfloat16 [2304, 9216], P('fsdp'), may hold values from -0.125 to 0.125
- down_weight: bfloat16 [9216, 2304], P('fsdp'), may hold values from -0.0625 to 0.0625
- pre_attention_gain: float32 [2304], replicated, may hold values from 0.25 to 1.75
- post_attention_gain: float32 [2304], replicated, may hold values from 0.25 to 1.75
- pre_feedforward_gain: float32 [2304], replicated, may hold values from 0.25 to 1.75
- post_feedforward_gain: float32 [2304], replicated, may hold values from 0.25 to 1.75
Outputs:
- block_output: bfloat16 [4, 1024, 2304], P('fsdp', 'context')
- input_grad: bfloat16 [4, 1024, 2304], P('fsdp', 'context')
- query_weight_grad: float32 [2304, 2048], P(('fsdp', 'context'))
- key_weight_grad: float32 [2304, 1024], P(('fsdp', 'context'))
- value_weight_grad: float32 [2304, 1024], P(('fsdp', 'context'))
- output_weight_grad: float32 [2048, 2304], P(('fsdp', 'context'))
- gate_weight_grad: float32 [2304, 9216], P(('fsdp', 'context'))
- up_weight_grad: float32 [2304, 9216], P(('fsdp', 'context'))
- down_weight_grad: float32 [9216, 2304], P(('fsdp', 'context'))
- pre_attention_gain_grad: float32 [2304], P(('fsdp', 'context'))
- post_attention_gain_grad: float32 [2304], P(('fsdp', 'context'))
- pre_feedforward_gain_grad: float32 [2304], P(('fsdp', 'context'))
- post_feedforward_gain_grad: float32 [2304], P(('fsdp', 'context'))
The draws below stay inside these ranges and needn't reach their ends.
Inputs may be any that keep to these rules, and one draw needn't show every extreme that they name: `block_table`: row c gives the two blocks of every sequence stored at index c of context: some block b and the block 15 - b; each of the 16 blocks appears exactly once.
All inputs are finite; a program needn't handle non-finite values.
Results may differ from the reference program's by a relative error of at most 0.02.
Values may be sent and summed in bfloat16 or wider, within the bound.
No kernel may reach another device: no remote copies, remote signals or barrier semaphores. Data moves between devices by JAX's collectives and lax.ppermute only.
A program may use at most 512 MiB of HBM per device.

```python
import math
import jax
import jax.numpy as jnp
from jax import lax

D = 2304
HEADS = 8
KV_HEADS = 4
HEAD_DIM = 256
FF = 9216
BLOCK = 64
SEQ_LEN = 1024
SEQS = 4
BLOCKS = 16


def draw_block_table(key, part):
    shuffled = jax.random.permutation(key, BLOCKS // 2).astype(jnp.int32)
    return jnp.stack([shuffled, BLOCKS - 1 - shuffled], axis=1).astype(jnp.int32)


def spiked(values, own_key, source, target, parts, factor):
    def block_of(position):
        return (jnp.arange(values.shape[position]) // (values.shape[position] // parts)).reshape((-1,) + (1,) * (values.ndim - 1 - position))

    first = jax.random.permutation(own_key, parts)[block_of(target)]
    far = (block_of(target) + parts // 2) % parts
    return jnp.where((block_of(source) == first) | (block_of(source) == far), factor * values, values)


def block_scale(key, extent, shards, low, largest):
    level, own = 1.0, jax.random.fold_in(key, 6)
    for dim, blocks in shards:
        heights = jnp.exp(jax.random.uniform(jax.random.fold_in(own, dim), (blocks,), jnp.float32, low / len(shards), largest / len(shards)))
        level = level * jnp.repeat(heights, extent[dim] // blocks).reshape([-1 if axis == dim else 1 for axis in range(len(extent))])
    return level


def bell_draw(stream_key, dims, spread, reach, pieces=(), kind=jnp.bfloat16):
    array = jax.random.normal(stream_key, dims, jnp.float32) * spread
    if len(pieces) > 0:
        array = block_scale(stream_key, dims, pieces, -0.22, 0.18) * array
    return jnp.clip(array, min=-reach, max=reach).astype(kind)


def noise_with(stream_key, dims, scale, most, shards, heavy, kind=jnp.bfloat16):
    entries = scale * jax.random.normal(stream_key, dims, jnp.float32)
    if shards:
        entries = entries * block_scale(stream_key, dims, shards, -0.22, 0.18)
    return jnp.clip(spiked(entries, jax.random.fold_in(stream_key, 3), *heavy), -most, most).astype(kind)


def setup_inputs(seed: int = 0) -> dict:
    seeds = jax.random.split(jax.random.key(seed), 15)
    return {
        "block_table": draw_block_table(jax.random.fold_in(seeds[14], 71), 0),
        "block_input": noise_with(seeds[1], (SEQS, SEQ_LEN, D), 1.0, 6.0, ((0, 4), (1, 8)), (1, 2, 8, 2.0)),
        "output_grad": bell_draw(seeds[2], (SEQS, SEQ_LEN, D), 1.0, 6.0, ((0, 4), (1, 8))),
        "query_weight": bell_draw(seeds[3], (D, HEADS * HEAD_DIM), D ** -0.5, 0.125, ((0, 4),)),
        "key_weight": bell_draw(seeds[4], (D, KV_HEADS * HEAD_DIM), D ** -0.5, 0.125, ((0, 4),)),
        "value_weight": bell_draw(seeds[5], (D, KV_HEADS * HEAD_DIM), D ** -0.5, 0.125, ((0, 4),)),
        "output_weight": bell_draw(seeds[6], (HEADS * HEAD_DIM, D), (HEADS * HEAD_DIM) ** -0.5, 0.125, ((0, 4),)),
        "gate_weight": bell_draw(seeds[7], (D, FF), D ** -0.5, 0.125, ((0, 4),)),
        "up_weight": bell_draw(seeds[8], (D, FF), D ** -0.5, 0.125, ((0, 4),)),
        "down_weight": bell_draw(seeds[9], (FF, D), FF ** -0.5, 0.0625, ((0, 4),)),
        "pre_attention_gain": jnp.clip(1.0 + 0.15 * jax.random.normal(seeds[10], (D,), jnp.float32), 0.25, 1.75),
        "post_attention_gain": jnp.clip(1.0 + 0.15 * jax.random.normal(seeds[11], (D,), jnp.float32), 0.25, 1.75),
        "pre_feedforward_gain": jnp.clip(1.0 + 0.15 * jax.random.normal(seeds[12], (D,), jnp.float32), 0.25, 1.75),
        "post_feedforward_gain": jnp.clip(1.0 + 0.15 * jax.random.normal(seeds[13], (D,), jnp.float32), 0.25, 1.75),
    }


EPSILON = 1e-06
SOFT_CAP = 50.0
GELU_COEF = 0.044715
ROOT_TWO_PI = math.sqrt(2.0 / math.pi)

def row_scale(matrix):
    return lax.rsqrt(lax.optimization_barrier(jnp.mean(matrix * matrix, axis=-1, keepdims=True)) + EPSILON)

def norm_back(source, scales, gain, upstream):
    weighted = upstream * gain
    inner = lax.optimization_barrier(jnp.mean(weighted * source, axis=-1, keepdims=True))
    result = scales * weighted - source * (scales * scales * scales) * inner
    return (result, lax.optimization_barrier(jnp.sum(upstream * source * scales, axis=0)))

def gelu_value(inputs):
    inner = ROOT_TWO_PI * (inputs + GELU_COEF * inputs * inputs * inputs)
    return 0.5 * inputs * (1.0 + jnp.tanh(inner))

def gelu_slope(inputs):
    tangent = jnp.tanh(ROOT_TWO_PI * (inputs + GELU_COEF * inputs * inputs * inputs))
    return 0.5 * (1.0 + tangent) + 0.5 * inputs * (1.0 - tangent * tangent) * ROOT_TWO_PI * (1.0 + 3.0 * GELU_COEF * inputs * inputs)

def rotary_tables(positions):
    half_dim = HEAD_DIM // 2
    frequency = jnp.exp(jnp.arange(half_dim, dtype=jnp.float32) * (-2.0 * math.log(10000.0) / HEAD_DIM))
    angles = positions.astype(jnp.float32)[:, None] * frequency[None, :]
    return (jnp.cos(angles), jnp.sin(angles))

def rotate(heads_rows, cosine, sine, direction):
    half_dim = heads_rows.shape[-1] // 2
    first_half = heads_rows[..., :half_dim]
    second_half = heads_rows[..., half_dim:]
    cosine = cosine[:, None, :]
    sine = sine[:, None, :]
    return jnp.concatenate([first_half * cosine - direction * second_half * sine, second_half * cosine + direction * first_half * sine], axis=-1)

def grouped(heads_rows):
    row_count = heads_rows.shape[0]
    group_size = HEADS // KV_HEADS
    return heads_rows.reshape(row_count, KV_HEADS, group_size, HEAD_DIM).transpose(1, 2, 0, 3).reshape(KV_HEADS, group_size * row_count, HEAD_DIM)

def ungrouped(grouped_rows, row_count):
    group_size = HEADS // KV_HEADS
    return grouped_rows.reshape(KV_HEADS, group_size, row_count, HEAD_DIM).transpose(2, 0, 1, 3).reshape(row_count, HEADS * HEAD_DIM)

def wide_einsum(form, left, right):
    return jnp.einsum(form, left.astype(jnp.float32), right.astype(jnp.float32))

def capped_scores(query_group, key_heads, query_positions, key_positions):
    raw = wide_einsum('grd,kgd->grk', query_group, key_heads) * (1.0 / math.sqrt(HEAD_DIM))
    capped = SOFT_CAP * jnp.tanh(raw / SOFT_CAP)
    group_size = HEADS // KV_HEADS
    allowed = key_positions[None, :] <= jnp.tile(query_positions, group_size)[:, None]
    return (capped, allowed)

def attend_forward(queries, query_positions, key_heads, value_heads, key_positions):
    row_count = queries.shape[0]
    query_group = grouped(queries)
    capped, allowed = capped_scores(query_group, key_heads, query_positions, key_positions)
    masked = jnp.where(allowed[None], capped, -1e+30)
    highest = lax.optimization_barrier(jnp.max(masked, axis=-1, keepdims=True))
    logsum = highest + jnp.log(lax.optimization_barrier(jnp.sum(jnp.exp(masked - highest), axis=-1, keepdims=True)))
    attention = jnp.exp(masked - logsum).astype(jnp.bfloat16)
    combined = wide_einsum('grk,kgd->grd', attention, value_heads)
    return (ungrouped(combined, row_count).astype(jnp.bfloat16), logsum)

def attend_backward(queries, query_positions, key_heads, value_heads, key_positions, attended, logsum, attended_grad):
    row_count = queries.shape[0]
    query_group = grouped(queries)
    capped, allowed = capped_scores(query_group, key_heads, query_positions, key_positions)
    masked = jnp.where(allowed[None], capped, -1e+30)
    attention = jnp.exp(masked - logsum)
    attention_low = attention.astype(jnp.bfloat16)
    grad_group = grouped(attended_grad.reshape(row_count, HEADS, HEAD_DIM))
    attended_group = grouped(attended.reshape(row_count, HEADS, HEAD_DIM))
    delta = lax.optimization_barrier(jnp.sum(grad_group.astype(jnp.float32) * attended_group.astype(jnp.float32), axis=-1, keepdims=True))
    through = wide_einsum('grd,kgd->grk', grad_group, value_heads)
    ratio = capped / SOFT_CAP
    score_grad = (attention * (through - delta) * (1.0 - ratio * ratio) * (1.0 / math.sqrt(HEAD_DIM))).astype(jnp.bfloat16)
    query_grad = ungrouped(wide_einsum('grk,kgd->grd', score_grad, key_heads), row_count)
    key_grad = wide_einsum('grk,grd->kgd', score_grad, query_group).reshape(-1, KV_HEADS * HEAD_DIM)
    value_grad = wide_einsum('grk,grd->kgd', attention_low, grad_group).reshape(-1, KV_HEADS * HEAD_DIM)
    return (query_grad, key_grad, value_grad)

def matmul(left, right):
    return jnp.dot(left, right, preferred_element_type=jnp.float32)

def reference(block_table, block_input, output_grad, query_weight, key_weight, value_weight, output_weight, gate_weight, up_weight, down_weight, pre_attention_gain, post_attention_gain, pre_feedforward_gain, post_feedforward_gain):
    seq_len = block_input.shape[1]
    positions = (jnp.repeat(block_table.reshape(-1), BLOCK) * BLOCK + jnp.tile(jnp.arange(BLOCK, dtype=jnp.int32), block_table.size)).astype(jnp.int32)
    cosine, sine = rotary_tables(positions)
    span = math.gcd(512, seq_len)
    count = seq_len // span
    position_blocks = positions.reshape(count, span)

    def sequence_step(totals, pair):
        tokens = pair[0].astype(jnp.float32)
        cotangent = pair[1].astype(jnp.float32)
        scale_one = row_scale(tokens)
        normed = (tokens * scale_one * pre_attention_gain).astype(jnp.bfloat16)
        queries = rotate(matmul(normed, query_weight).reshape(seq_len, HEADS, HEAD_DIM), cosine, sine, 1.0).astype(jnp.bfloat16)
        key_heads = rotate(matmul(normed, key_weight).reshape(seq_len, KV_HEADS, HEAD_DIM), cosine, sine, 1.0).astype(jnp.bfloat16)
        value_heads = matmul(normed, value_weight).astype(jnp.bfloat16).reshape(seq_len, KV_HEADS, HEAD_DIM)
        query_blocks = queries.reshape(count, span, HEADS, HEAD_DIM)

        def forward_block(item):
            return attend_forward(item[0], item[1], key_heads, value_heads, positions)
        attended_blocks, logsum_blocks = lax.map(forward_block, (query_blocks, position_blocks))
        attended = attended_blocks.reshape(seq_len, HEADS * HEAD_DIM)
        attention_branch = matmul(attended, output_weight)
        scale_two = row_scale(attention_branch)
        middle = tokens + attention_branch * scale_two * post_attention_gain
        scale_three = row_scale(middle)
        normed_middle = (middle * scale_three * pre_feedforward_gain).astype(jnp.bfloat16)
        gate = matmul(normed_middle, gate_weight)
        upward = matmul(normed_middle, up_weight)
        activated = gelu_value(gate)
        hidden = (activated * upward).astype(jnp.bfloat16)
        feedforward_branch = matmul(hidden, down_weight)
        scale_four = row_scale(feedforward_branch)
        result = (middle + feedforward_branch * scale_four * post_feedforward_gain).astype(jnp.bfloat16)
        feed_grad, gain_four = norm_back(feedforward_branch, scale_four, post_feedforward_gain, cotangent)
        feed_low = feed_grad.astype(jnp.bfloat16)
        hidden_grad = matmul(feed_low, down_weight.T)
        gate_grad = (hidden_grad * upward * gelu_slope(gate)).astype(jnp.bfloat16)
        up_grad = (hidden_grad * activated).astype(jnp.bfloat16)
        normed_middle_grad = matmul(gate_grad, gate_weight.T) + matmul(up_grad, up_weight.T)
        middle_part, gain_three = norm_back(middle, scale_three, pre_feedforward_gain, normed_middle_grad)
        middle_grad = cotangent + middle_part
        branch_grad, gain_two = norm_back(attention_branch, scale_two, post_attention_gain, middle_grad)
        branch_low = branch_grad.astype(jnp.bfloat16)
        attended_grad = matmul(branch_low, output_weight.T).astype(jnp.bfloat16)
        grad_blocks = attended_grad.reshape(count, span, HEADS * HEAD_DIM)
        empty = jnp.zeros((seq_len, KV_HEADS * HEAD_DIM), jnp.float32)

        def backward_block(carry, item):
            query_grad, key_grad, value_grad = attend_backward(item[0], item[1], key_heads, value_heads, positions, item[2], item[3], item[4])
            return ((carry[0] + key_grad, carry[1] + value_grad), query_grad)
        (key_total, value_total), query_grads = lax.scan(backward_block, (empty, empty), (query_blocks, position_blocks, attended_blocks, logsum_blocks, grad_blocks))
        query_low = rotate(query_grads.reshape(seq_len, HEADS, HEAD_DIM), cosine, sine, -1.0).reshape(seq_len, HEADS * HEAD_DIM).astype(jnp.bfloat16)
        key_low = rotate(key_total.reshape(seq_len, KV_HEADS, HEAD_DIM), cosine, sine, -1.0).reshape(seq_len, KV_HEADS * HEAD_DIM).astype(jnp.bfloat16)
        value_low = value_total.astype(jnp.bfloat16)
        normed_grad = matmul(query_low, query_weight.T) + matmul(key_low, key_weight.T) + matmul(value_low, value_weight.T)
        token_part, gain_one = norm_back(tokens, scale_one, pre_attention_gain, normed_grad)
        input_grad = (middle_grad + token_part).astype(jnp.bfloat16)
        terms = (matmul(normed.T, query_low), matmul(normed.T, key_low), matmul(normed.T, value_low), matmul(attended.T, branch_low), matmul(normed_middle.T, gate_grad), matmul(normed_middle.T, up_grad), matmul(hidden.T, feed_low), gain_one, gain_two, gain_three, gain_four)
        return (jax.tree.map(jnp.add, totals, terms), (result, input_grad))
    starting = (jnp.zeros(query_weight.shape, jnp.float32), jnp.zeros(key_weight.shape, jnp.float32), jnp.zeros(value_weight.shape, jnp.float32), jnp.zeros(output_weight.shape, jnp.float32), jnp.zeros(gate_weight.shape, jnp.float32), jnp.zeros(up_weight.shape, jnp.float32), jnp.zeros(down_weight.shape, jnp.float32), jnp.zeros((D,), jnp.float32), jnp.zeros((D,), jnp.float32), jnp.zeros((D,), jnp.float32), jnp.zeros((D,), jnp.float32))
    totals, (outputs, input_grads) = lax.scan(sequence_step, starting, (block_input, output_grad))
    return (outputs, input_grads, totals[0], totals[1], totals[2], totals[3], totals[4], totals[5], totals[6], totals[7], totals[8], totals[9], totals[10])
```

```python
import math

import jax
import jax.numpy as jnp
from jax import lax
from jax.sharding import PartitionSpec as P

HEADS = 8
HEAD_DIM = 256
BLOCK = 64


EPSILON = 1e-06
SOFT_CAP = 50.0
GELU_COEF = 0.044715
ROOT_TWO_PI = math.sqrt(2.0 / math.pi)

AXES = ("fsdp", "context")
SUBLANES = 8


def row_scale(matrix):
    return lax.rsqrt(jnp.mean(matrix * matrix, axis=-1, keepdims=True) + EPSILON)


def norm_back(source, scales, gain, upstream):
    weighted = upstream * gain
    inner = jnp.mean(weighted * source, axis=-1, keepdims=True)
    result = scales * weighted - source * (scales * scales * scales) * inner
    return (result, jnp.sum(upstream * source * scales, axis=0))


def gelu_parts(inputs):
    tangent = jnp.tanh(ROOT_TWO_PI * (inputs + GELU_COEF * inputs * inputs * inputs))
    value = 0.5 * inputs * (1.0 + tangent)
    slope = 0.5 * (1.0 + tangent) + 0.5 * inputs * (1.0 - tangent * tangent) * ROOT_TWO_PI * (
        1.0 + 3.0 * GELU_COEF * inputs * inputs
    )
    return (value, slope)


def rotary_tables(positions):
    half_dim = HEAD_DIM // 2
    frequency = jnp.exp(
        jnp.arange(half_dim, dtype=jnp.float32) * (-2.0 * math.log(10000.0) / HEAD_DIM)
    )
    angles = positions.astype(jnp.float32)[:, None] * frequency[None, :]
    return (jnp.cos(angles), jnp.sin(angles))


def rotate(rows, cosine, sine, direction):
    half_dim = rows.shape[-1] // 2
    first_half = rows[..., :half_dim]
    second_half = rows[..., half_dim:]
    return jnp.concatenate(
        [
            first_half * cosine - direction * second_half * sine,
            second_half * cosine + direction * first_half * sine,
        ],
        axis=-1,
    )


def dot_rows(left, right):
    return jnp.dot(left, right, preferred_element_type=jnp.float32)


def dot_columns(left, right):
    return lax.dot_general(
        left, right, (((1,), (1,)), ((), ())), preferred_element_type=jnp.float32
    )


def dot_tokens(left, right):
    return lax.dot_general(
        left, right, (((0,), (0,)), ((), ())), preferred_element_type=jnp.float32
    )


def einsum(form, left, right):
    return jnp.einsum(form, left, right, preferred_element_type=jnp.float32)


def low(values):
    return values.astype(jnp.bfloat16)


def wide(values):
    return values.astype(jnp.float32)


class Grid:
    def __init__(self):
        self.context = lax.axis_size("context")
        self.count = lax.axis_size("fsdp") * self.context
        self.number = lax.axis_index("fsdp") * self.context + lax.axis_index("context")
        self.core = self.context
        self.x = 2 * self.context
        self.y = 1
        self.z = [1 << i for i in range(1, self.context.bit_length() - 1)]
        self.order = [1 << i for i in reversed(range(self.count.bit_length() - 1))]

    def bit(self, mask, number=None):
        number = self.number if number is None else number
        return (number // mask) % 2

    def swap(self, values, mask):
        return lax.ppermute(values, AXES, [(i, i ^ mask) for i in range(self.count)])

    def send(self, values, target):
        return lax.ppermute(values, AXES, [(i, target(i)) for i in range(self.count)])

    def spread(self, piece, order):
        pieces = {0: piece}
        for mask in order:
            pieces.update({held | mask: self.swap(v, mask) for held, v in list(pieces.items())})
        return pieces

    def collect(self, pieces, order):
        for mask in reversed(order):
            arrived = {k: self.swap(v, mask) for k, v in pieces.items() if k & mask}
            kept = {k: v for k, v in pieces.items() if not k & mask}
            pieces = {k: wide(v) + wide(arrived[k | mask]) for k, v in kept.items()}
            if len(pieces) > 1:
                pieces = {k: low(v) for k, v in pieces.items()}
        return pieces[0]

    def halve(self, terms, masks, axes):
        axes = list(axes)
        for mask in masks:
            place = axes.index(mask)
            mine = self.bit(mask)
            away = lax.dynamic_index_in_dim(terms, 1 - mine, place, keepdims=False)
            kept = lax.dynamic_index_in_dim(terms, mine, place, keepdims=False)
            total = wide(kept) + wide(self.swap(away, mask))
            terms = total.astype(terms.dtype)
            axes.remove(mask)
        return terms

    def exchange(self, blocks, masks, shard_of):
        size = 1 << len(masks)
        lead = len(masks)

        def block_at(offset):
            start = [self.bit(m, self.number ^ offset) for m in masks] + [0, 0]
            piece = lax.dynamic_slice(blocks, start, (1,) * lead + blocks.shape[lead:])
            return piece.reshape(blocks.shape[lead:])

        out = jnp.zeros((size,) + blocks.shape[lead:], blocks.dtype)
        for i in range(size):
            offset = sum(m for j, m in enumerate(masks) if i >> j & 1)
            piece = block_at(offset)
            if offset:
                piece = self.swap(piece, offset)
            out = lax.dynamic_update_slice(
                out, piece[None], (shard_of(self.number ^ offset), 0, 0)
            )
        return out


def thirds(rows):
    units = rows // SUBLANES
    cuts = [0, (units + 2) // 3 * SUBLANES, 0, rows]
    cuts[2] = cuts[1] + (units - cuts[1] // SUBLANES + 1) // 2 * SUBLANES
    return [(cuts[i], cuts[i + 1]) for i in range(3)]


class Cube:
    def __init__(self, grid, rows):
        x, y, z = grid.x, grid.y, grid.z[0]
        self.grid = grid
        self.parts = list(zip(thirds(rows), ((x, y, z), (y, z, x), (z, x, y)), strict=True))
        self.masks = [
            sum(m for j, m in enumerate((x, y, z)) if i >> j & 1) for i in range(8)
        ]

    def gather(self, own):
        out = []
        for (start, end), order in self.parts:
            pieces = self.grid.spread(own[start:end], order)
            out += [pieces[m] for m in self.masks]
        return jnp.concatenate(out, axis=0)

    def scatter(self, terms):
        out, place = [], 0
        for (start, end), order in self.parts:
            pieces = {}
            for m in self.masks:
                pieces[m] = terms[place : place + end - start]
                place += end - start
            out.append(self.grid.collect(pieces, order))
        return jnp.concatenate(out, axis=0)


class Square:
    def __init__(self, grid, rows):
        self.grid = grid
        self.half = rows // 2
        self.orders = ((grid.x, grid.y), (grid.y, grid.x))
        self.keys = [
            (jx * grid.x, h, jy * grid.y) for jx in range(2) for h in range(2) for jy in range(2)
        ]

    def gather(self, own):
        core = self.grid.core
        found = [
            self.grid.spread(own[h * self.half : (h + 1) * self.half], self.orders[h] + (core,))
            for h in range(2)
        ]
        return jnp.concatenate(
            [found[h][jk | jx | jy] for jk in (0, core) for jx, h, jy in self.keys], axis=0
        )

    def scatter(self, near, far):
        arrived = self.grid.swap(far, self.grid.core)
        sums = [{}, {}]
        for i, (jx, h, jy) in enumerate(self.keys):
            rows = slice(i * self.half, (i + 1) * self.half)
            sums[h][jx | jy] = low(wide(near[rows]) + wide(arrived[rows]))
        return jnp.concatenate(
            [self.grid.collect(sums[h], self.orders[h]) for h in range(2)], axis=0
        )


def capped_scores(queries, keys, allowed):
    raw = einsum("sqd,skd->sqk", queries, keys) * (1.0 / math.sqrt(HEAD_DIM))
    capped = SOFT_CAP * jnp.tanh(raw / SOFT_CAP)
    return (capped, jnp.where(allowed[None], capped, -1e30))


def attend_forward(queries, keys, values, allowed):
    _, masked = capped_scores(queries, keys, allowed)
    highest = jnp.max(masked, axis=-1, keepdims=True)
    logsum = highest + jnp.log(jnp.sum(jnp.exp(masked - highest), axis=-1, keepdims=True))
    attention = low(jnp.exp(masked - logsum))
    return (low(einsum("sqk,skd->sqd", attention, values)), logsum)


def attend_backward(queries, keys, values, allowed, attended, logsum, attended_grad):
    capped, masked = capped_scores(queries, keys, allowed)
    attention = jnp.exp(masked - logsum)
    delta = jnp.sum(wide(attended_grad) * wide(attended), axis=-1, keepdims=True)
    through = einsum("sqd,skd->sqk", attended_grad, values)
    ratio = capped / SOFT_CAP
    score_grad = low(
        attention * (through - delta) * (1.0 - ratio * ratio) * (1.0 / math.sqrt(HEAD_DIM))
    )
    query_grad = einsum("sqk,skd->sqd", score_grad, keys)
    key_grad = einsum("sqk,sqd->skd", score_grad, queries)
    value_grad = einsum("sqk,sqd->skd", low(attention), attended_grad)
    return (query_grad, key_grad, value_grad)


def stacked_rows(grid, own, masks):
    shape = own[0].shape
    whole = jnp.zeros((len(own),) + shape, own[0].dtype)
    for piece, mask in zip(own, masks, strict=True):
        place = (grid.number ^ mask) // grid.context
        whole = lax.dynamic_update_slice(whole, piece[None], (place, 0, 0))
    return whole.reshape(len(own) * shape[0], shape[1])


def columns_at(matrix, index, width):
    return lax.dynamic_slice_in_dim(matrix, index * width, width, 1)


def shards(
    block_table,
    block_input,
    output_grad,
    query_weight,
    key_weight,
    value_weight,
    output_weight,
    gate_weight,
    up_weight,
    down_weight,
    pre_attention_gain,
    post_attention_gain,
    pre_feedforward_gain,
    post_feedforward_gain,
):
    grid = Grid()
    rows = block_input.shape[1]
    width = block_input.shape[2]
    feed = gate_weight.shape[1]
    x, core, y, z_masks = grid.x, grid.core, grid.y, grid.z
    bit_x, bit_core, bit_y, bit_z = (grid.bit(m) for m in (x, core, y, z_masks[0]))
    cube = Cube(grid, rows)
    square = Square(grid, rows)

    tokens_low = block_input[0]
    gathered = square.gather(tokens_low)

    def attention_columns(chip_x):
        chip = 2 * chip_x + bit_y
        pair = [columns_at(query_weight, 2 * chip + c, HEAD_DIM) for c in (bit_core, 1 - bit_core)]
        return pair + [
            columns_at(key_weight, chip, HEAD_DIM),
            columns_at(value_weight, chip, HEAD_DIM),
        ]

    def for_cores(parts):
        mine, other, key_part, value_part = parts
        return (
            jnp.concatenate([mine, key_part, value_part], axis=1),
            jnp.concatenate([other, key_part, value_part], axis=1),
        )

    near = for_cores(attention_columns(bit_x))
    away_x = grid.swap(jnp.concatenate(attention_columns(1 - bit_x), axis=1), x)
    far = for_cores([away_x[:, i * HEAD_DIM : (i + 1) * HEAD_DIM] for i in range(4)])
    projection = stacked_rows(
        grid,
        [near[0], grid.swap(near[1], core), far[0], grid.swap(far[1], core)],
        [0, core, x, x | core],
    )
    query_part = projection[:, :HEAD_DIM]
    pair_part = projection[:, HEAD_DIM:]

    head_rows = output_weight.shape[0] // 2
    output_rows = [
        lax.dynamic_slice_in_dim(output_weight, c * head_rows, head_rows, 0)
        for c in (bit_core, 1 - bit_core)
    ]
    output_part = jnp.where(bit_core == bit_y, output_rows[0], grid.swap(output_rows[1], core))

    feed_share = feed // 8
    shard = 4 * bit_x + 2 * bit_y + bit_z

    def feed_columns(index):
        return jnp.concatenate(
            [columns_at(gate_weight, index, feed_share), columns_at(up_weight, index, feed_share)],
            axis=1,
        )

    feed_near = feed_columns(shard)
    feed_far = grid.swap(feed_columns(shard + 4 * (1 - 2 * bit_x)), x)
    feed_in = stacked_rows(
        grid,
        [feed_near, grid.swap(feed_near, core), feed_far, grid.swap(feed_far, core)],
        [0, core, x, x | core],
    )
    down_rows = lax.dynamic_slice_in_dim(down_weight, bit_z * feed_share, feed_share, 0)
    down_part = jnp.where(bit_core == bit_y, down_rows, grid.swap(down_rows, core))

    offsets = jnp.arange(BLOCK, dtype=jnp.int32)

    def positions_at(mask):
        held = [
            lax.dynamic_index_in_dim(
                block_table, (grid.number ^ mask ^ m) % grid.context, 0, keepdims=False
            )
            for m in (0, y)
        ]
        return jnp.concatenate([pair[h] * BLOCK + offsets for h in range(2) for pair in held])

    z_order = list(reversed(z_masks))
    z_offsets = [0]
    for mask in z_order:
        z_offsets += [held | mask for held in z_offsets]
    query_positions = positions_at(0)
    key_positions = jnp.concatenate([positions_at(m) for m in z_offsets])
    allowed = key_positions[None, :] <= query_positions[:, None]
    cosine, sine = rotary_tables(query_positions)

    span = 2 * rows
    seqs = gathered.shape[0] // span
    own_rows = gathered.shape[0] // 2

    gathered_wide = wide(gathered)
    normed = low(gathered_wide * row_scale(gathered_wide) * pre_attention_gain)
    pair_own = dot_rows(normed[:own_rows], pair_part).reshape(seqs // 2, span, 2 * HEAD_DIM)
    pair_low = jnp.concatenate(
        [
            low(rotate(pair_own[..., :HEAD_DIM], cosine, sine, 1.0)),
            low(pair_own[..., HEAD_DIM:]),
        ],
        axis=-1,
    )
    pairs_z = grid.spread(pair_low, z_order)
    queries = low(
        rotate(dot_rows(normed, query_part).reshape(seqs, span, HEAD_DIM), cosine, sine, 1.0)
    )
    pair_sets = [pairs_z[m] for m in z_offsets]
    pair_sets_other = [grid.swap(p, core) for p in pair_sets]
    pairs = jnp.concatenate(
        [jnp.concatenate(pair_sets, axis=1), jnp.concatenate(pair_sets_other, axis=1)], axis=0
    )
    keys, values = pairs[..., :HEAD_DIM], pairs[..., HEAD_DIM:]
    attended, logsum = attend_forward(queries, keys, values, allowed)
    attended_rows = attended.reshape(-1, HEAD_DIM)
    branch_far = low(dot_rows(attended_rows[own_rows:], output_part))
    branch_near = low(dot_rows(attended_rows[:own_rows], output_part))
    attention_branch = square.scatter(branch_near, branch_far)

    tokens = wide(tokens_low)
    cotangent = wide(output_grad[0])
    scale_two = row_scale(attention_branch)
    middle = tokens + attention_branch * scale_two * post_attention_gain
    scale_three = row_scale(middle)
    normed_middle = cube.gather(low(middle * scale_three * pre_feedforward_gain))

    both = dot_rows(normed_middle, feed_in)
    gate, upward = both[:, :feed_share], both[:, feed_share:]
    activated, slope = gelu_parts(gate)
    hidden = low(activated * upward)
    feedforward_branch = cube.scatter(low(dot_rows(hidden, down_part)))
    scale_four = row_scale(feedforward_branch)
    result = low(middle + feedforward_branch * scale_four * post_feedforward_gain)
    feed_grad, gain_four = norm_back(
        feedforward_branch, scale_four, post_feedforward_gain, cotangent
    )
    feed_low = cube.gather(low(feed_grad))
    hidden_grad = dot_columns(feed_low, down_part)
    both_grad = jnp.concatenate(
        [low(hidden_grad * upward * slope), low(hidden_grad * activated)], axis=1
    )
    normed_middle_grad = cube.scatter(low(dot_columns(both_grad, feed_in)))
    down_terms = low(dot_tokens(hidden, feed_low))
    feed_terms = low(dot_tokens(normed_middle, both_grad))

    middle_part, gain_three = norm_back(
        middle, scale_three, pre_feedforward_gain, normed_middle_grad
    )
    middle_grad = cotangent + middle_part
    branch_grad, gain_two = norm_back(attention_branch, scale_two, post_attention_gain, middle_grad)
    branch_low = square.gather(low(branch_grad))
    attended_grad = low(dot_columns(branch_low, output_part)).reshape(seqs, span, HEAD_DIM)
    output_terms = low(dot_tokens(attended_rows, branch_low))
    query_grad, key_grad, value_grad = attend_backward(
        queries, keys, values, allowed, attended, logsum, attended_grad
    )
    query_low = low(rotate(query_grad, cosine, sine, -1.0)).reshape(-1, HEAD_DIM)
    near_seqs = seqs // 2
    pair_terms = low(jnp.concatenate([key_grad, value_grad], axis=-1))
    pair_other = grid.swap(pair_terms[near_seqs:], core)
    pair_sum = low(wide(pair_terms[:near_seqs]) + wide(pair_other))
    pair_total = grid.collect(
        {m: pair_sum[:, i * span : (i + 1) * span] for i, m in enumerate(z_offsets)}, z_order
    )
    pair_grad = jnp.concatenate(
        [
            low(rotate(pair_total[..., :HEAD_DIM], cosine, sine, -1.0)),
            low(pair_total[..., HEAD_DIM:]),
        ],
        axis=-1,
    ).reshape(own_rows, 2 * HEAD_DIM)
    normed_far = low(dot_columns(query_low[own_rows:], query_part))
    normed_near = low(
        dot_columns(query_low[:own_rows], query_part) + dot_columns(pair_grad, pair_part)
    )
    normed_grad = square.scatter(normed_near, normed_far)
    scale_one = row_scale(tokens)
    token_part, gain_one = norm_back(tokens, scale_one, pre_attention_gain, normed_grad)
    input_grad = low(middle_grad + token_part)
    query_terms = low(dot_tokens(normed, query_low))
    pair_weight_terms = low(dot_tokens(normed[:own_rows], pair_grad))

    bits = grid.order
    lead = (2,) * len(bits)
    cube_masks = [x, z_masks[0], y]
    rest = [core] + z_masks[1:]

    def by_device(terms):
        return terms.reshape(lead + (terms.shape[0] // grid.count, terms.shape[1]))

    def shard_of(number):
        return 4 * grid.bit(x, number) + 2 * grid.bit(y, number) + grid.bit(z_masks[0], number)

    def chunk_of(number, masks):
        index = 0
        for mask in masks:
            index = 2 * index + number // mask % 2
        return index

    def to_owner(terms, masks, block_of):
        chunks = terms.reshape((2,) * len(masks) + (-1, terms.shape[1]))
        summed = grid.halve(chunks, masks, masks)
        size = 1 << len(masks)
        return grid.send(summed, lambda i: block_of(i) * size + chunk_of(i, masks))

    def side_by_side(blocks):
        return wide(blocks.transpose(1, 0, 2).reshape(blocks.shape[1], -1))

    down_sums = wide(to_owner(down_terms, rest, shard_of))
    feed_blocks = grid.exchange(
        grid.halve(by_device(feed_terms), rest, bits), cube_masks, shard_of
    )
    gate_sums = side_by_side(feed_blocks[..., :feed_share])
    up_sums = side_by_side(feed_blocks[..., feed_share:])

    def group_of(number):
        return 2 * grid.bit(x, number) + grid.bit(y, number)

    def head_of(number):
        return 2 * group_of(number) + grid.bit(core, number)

    output_sums = wide(to_owner(output_terms, z_masks, head_of))
    query_blocks = grid.exchange(
        grid.halve(by_device(query_terms), z_masks, bits), [x, core, y], head_of
    )
    pair_blocks = grid.exchange(
        grid.halve(by_device(pair_weight_terms), [core] + z_masks, bits), [x, y], group_of
    )
    gains = jnp.stack([gain_one, gain_two, gain_three, gain_four], axis=1)
    gain_sums = grid.halve(by_device(gains), list(reversed(bits)), bits)
    return (
        result[None],
        input_grad[None],
        side_by_side(query_blocks),
        side_by_side(pair_blocks[..., :HEAD_DIM]),
        side_by_side(pair_blocks[..., HEAD_DIM:]),
        output_sums,
        gate_sums,
        up_sums,
        down_sums,
        gain_sums[:, 0],
        gain_sums[:, 1],
        gain_sums[:, 2],
        gain_sums[:, 3],
    )


def solution(mesh):
    in_specs = (
        P(),
        P("fsdp", "context", None),
        P("fsdp", "context", None),
        P("fsdp", None),
        P("fsdp", None),
        P("fsdp", None),
        P("fsdp", None),
        P("fsdp", None),
        P("fsdp", None),
        P("fsdp", None),
        P(),
        P(),
        P(),
        P(),
    )
    out_specs = (
        P("fsdp", "context", None),
        P("fsdp", "context", None),
        P(("fsdp", "context"), None),
        P(("fsdp", "context"), None),
        P(("fsdp", "context"), None),
        P(("fsdp", "context"), None),
        P(("fsdp", "context"), None),
        P(("fsdp", "context"), None),
        P(("fsdp", "context"), None),
        P(("fsdp", "context")),
        P(("fsdp", "context")),
        P(("fsdp", "context")),
        P(("fsdp", "context")),
    )
    return jax.shard_map(shards, mesh=mesh, in_specs=in_specs, out_specs=out_specs, check_vma=False)
```
